32 devices in a mesh: seq: 4 (over x, core), fsdp: 8 (over z, y).
Axes of the slice: x: 2, y: 2, z: 4, core: 2. Of those that a mesh axis runs over, the one named last changes fastest.
Arguments:
- image_tokens: bfloat16 [8, 1024, 1536], P('fsdp', 'seq'), may hold values from -6 to 6
- text_tokens: bfloat16 [8, 160, 1536], P('fsdp', 'seq'), may hold values from -6 to 6
- condition: bfloat16 [8, 1536], P('fsdp'), may hold values from -6 to 6
- occupied: int32 [8], P('fsdp'), may hold values 0 or 1
- image_cotangent: bfloat16 [8, 1024, 1536], P('fsdp', 'seq'), may hold values from -6 to 6
- text_cotangent: bfloat16 [8, 160, 1536], P('fsdp', 'seq'), may hold values from -6 to 6
- image_modulator: bfloat16 [1, 1536, 9216], P(None, 'fsdp'), may hold values from -0.15625 to 0.15625
- image_heads: bfloat16 [1, 1536, 4608], P(None, 'fsdp'), may hold values from -0.21875 to 0.21875
- image_merge: bfloat16 [1, 1536, 1536], P(None, 'fsdp'), may hold values from -0.3125 to 0.3125
- image_expand: bfloat16 [1, 1536, 6144], P(None, 'fsdp'), may hold values from -0.15625 to 0.15625
- image_reduce: bfloat16 [1, 6144, 1536], P(None, 'fsdp'), may hold values from -0.078125 to 0.078125
- text_modulator: bfloat16 [1, 1536, 9216], P(None, 'fsdp'), may hold values from -0.15625 to 0.15625
- text_heads: bfloat16 [1, 1536, 4608], P(None, 'fsdp'), may hold values from -0.21875 to 0.21875
- text_merge: bfloat16 [1, 1536, 1536], P(None, 'fsdp'), may hold values from -0.3125 to 0.3125
- text_expand: bfloat16 [1, 1536, 6144], P(None, 'fsdp'), may hold values from -0.15625 to 0.15625
- text_reduce: bfloat16 [1, 6144, 1536], P(None, 'fsdp'), may hold values from -0.078125 to 0.078125
Outputs:
- image_output: bfloat16 [8, 1024, 1536], P('fsdp', 'seq')
- text_output: bfloat16 [8, 160, 1536], P('fsdp', 'seq')
- image_input_grad: bfloat16 [8, 1024, 1536], P('fsdp', 'seq')
- text_input_grad: bfloat16 [8, 160, 1536], P('fsdp', 'seq')
- condition_grad: float32 [8, 1536], P('fsdp')
- image_modulator_grad: float32 [1, 1536, 9216], P(None, 'fsdp')
- image_heads_grad: float32 [1, 1536, 4608], P(None, 'fsdp')
- image_merge_grad: float32 [1, 1536, 1536], P(None, 'fsdp')
- image_expand_grad: float32 [1, 1536, 6144], P(None, 'fsdp')
- image_reduce_grad: float32 [1, 6144, 1536], P(None, 'fsdp')
- text_modulator_grad: float32 [1, 1536, 9216], P(None, 'fsdp')
- text_heads_grad: float32 [1, 1536, 4608], P(None, 'fsdp')
- text_merge_grad: float32 [1, 1536, 1536], P(None, 'fsdp')
- text_expand_grad: float32 [1, 1536, 6144], P(None, 'fsdp')
- text_reduce_grad: float32 [1, 6144, 1536], P(None, 'fsdp')
The draws below stay inside these ranges and needn't reach their ends.
All inputs are finite; a program needn't handle non-finite values. No bound on the sum of `occupied` on one device may be relied on, other than what follows from the above.
Results may differ from the reference program's by a relative error of at most 0.02.
The reference program's roundings to bfloat16 on the way count: a program that leaves them out, or rounds other values in their place, can miss the bound.
Values may be sent and summed in bfloat16 or wider, within the bound.
No kernel may reach another device: no remote copies, remote signals or barrier semaphores. Data moves between devices by JAX's collectives and lax.ppermute only.
A program may use at most 448 MiB of HBM per device.

```python
import jax
import jax.numpy as jnp
from jax import lax

D = 1536
HEADS = 24
HEAD_DIM = 64
FF = 6144
LAYERS = 1
SEQS = 8
IMG = 1024
TXT = 160


def place_ends(drawn, key, low, high):
    place = [jax.random.randint(jax.random.fold_in(key, axis), (), 0, length) for axis, length in enumerate(drawn.shape)]
    widest = drawn.shape.index(max(drawn.shape))
    beside = place[:widest] + [(place[widest] + 1) % drawn.shape[widest]] + place[widest + 1:]
    return drawn.at[tuple(place)].set(low).at[tuple(beside)].set(high)


def levels(key, dims, cuts, smallest, high):
    level = 1.0
    for axis_at, shards_of in cuts:
        steps = jax.random.uniform(jax.random.fold_in(jax.random.fold_in(key, 6), axis_at), (shards_of,), jnp.float32, smallest / len(cuts), high / len(cuts))
        level = level * jnp.repeat(jnp.exp(steps), dims[axis_at] // shards_of).reshape((-1,) + (1,) * (len(dims) - 1 - axis_at))
    return level


def bell_draw(stream_key, extent, deviation, reach, cuts=(), kind=jnp.bfloat16):
    factor_of = levels(stream_key, extent, cuts, -0.22, 0.18) if cuts else 1.0
    array = jax.random.normal(stream_key, extent, jnp.float32) * deviation * factor_of
    return jnp.minimum(jnp.maximum(array, -reach), reach).astype(kind)


def setup_inputs(seed: int = 0) -> dict:
    key_list = jax.random.split(jax.random.key(seed), 17)
    return {
        "image_tokens": bell_draw(key_list[0], (SEQS, IMG, D), 1.0, 6.0, ((0, 8), (1, 4))),
        "text_tokens": bell_draw(key_list[1], (SEQS, TXT, D), 1.0, 6.0, ((0, 8), (1, 4))),
        "condition": bell_draw(key_list[2], (SEQS, D), 1.0, 6.0, ((0, 8),)),
        "occupied": place_ends((jax.random.randint(key_list[3], (SEQS,), 0, 32) < 27).astype(jnp.int32), jax.random.fold_in(key_list[3], 1), 0, 1),
        "image_cotangent": bell_draw(key_list[4], (SEQS, IMG, D), 1.0, 6.0, ((0, 8), (1, 4))),
        "text_cotangent": bell_draw(key_list[5], (SEQS, TXT, D), 1.0, 6.0, ((0, 8), (1, 4))),
        "image_modulator": bell_draw(key_list[6], (LAYERS, D, 6 * D), D ** -0.5, 0.15625, ((1, 8),)),
        "image_heads": bell_draw(key_list[7], (LAYERS, D, 3 * D), (D // 2) ** -0.5, 0.21875, ((1, 8),)),
        "image_merge": bell_draw(key_list[8], (LAYERS, D, D), (D // 4) ** -0.5, 0.3125, ((1, 8),)),
        "image_expand": bell_draw(key_list[9], (LAYERS, D, FF), D ** -0.5, 0.15625, ((1, 8),)),
        "image_reduce": bell_draw(key_list[10], (LAYERS, FF, D), FF ** -0.5, 0.078125, ((1, 8),)),
        "text_modulator": bell_draw(key_list[11], (LAYERS, D, 6 * D), D ** -0.5, 0.15625, ((1, 8),)),
        "text_heads": bell_draw(key_list[12], (LAYERS, D, 3 * D), (D // 2) ** -0.5, 0.21875, ((1, 8),)),
        "text_merge": bell_draw(key_list[13], (LAYERS, D, D), (D // 4) ** -0.5, 0.3125, ((1, 8),)),
        "text_expand": bell_draw(key_list[14], (LAYERS, D, FF), D ** -0.5, 0.15625, ((1, 8),)),
        "text_reduce": bell_draw(key_list[15], (LAYERS, FF, D), FF ** -0.5, 0.078125, ((1, 8),)),
    }


EPSILON = 1e-06
HIGHEST = lax.Precision.HIGHEST

@jax.custom_vjp
def low(v):
    return lax.optimization_barrier(v.astype(jnp.bfloat16)).astype(jnp.float32)

@jax.custom_vjp
def low_back(v):
    return v

def low_keep(v):
    return (low(v), None)

def low_pass(kept, grad):
    return (grad,)

def back_keep(v):
    return (v, None)

def back_low(kept, grad):
    return (low(grad),)
low.defvjp(low_keep, low_pass)
low_back.defvjp(back_keep, back_low)

def product(former, latter):
    return jnp.dot(former, latter, precision=HIGHEST, preferred_element_type=jnp.float32)

def layer_norm(values):
    centered = values - lax.optimization_barrier(jnp.mean(values, axis=-1, keepdims=True))
    return centered * lax.rsqrt(lax.optimization_barrier(jnp.mean(centered * centered, axis=-1, keepdims=True)) + EPSILON)

def joint_layer(hidden, modulation, weights):
    portions = [jnp.split(modulation[stream], 6) for stream in range(2)]
    projected = []
    for stream in range(2):
        portion = portions[stream]
        entry = low(layer_norm(hidden[stream]) * (1.0 + portion[1]) + portion[0])
        projected.append(low_back(low(product(entry, weights[4 * stream]))))
    joined = jnp.concatenate(projected, 0)
    length = joined.shape[0]
    grouped = joined.reshape(length, 3, HEADS, HEAD_DIM)
    scores = jnp.einsum('qhd,khd->hqk', grouped[:, 0], grouped[:, 1], precision=HIGHEST)
    scores = low_back(scores * HEAD_DIM ** (-0.5))
    probs = jax.nn.softmax(scores, axis=-1)
    attended = jnp.einsum('hqk,khd->qhd', low(probs), grouped[:, 2], precision=HIGHEST)
    attended = low_back(low(attended.reshape(length, D)))
    image_count = hidden[0].shape[0]
    pieces = (attended[:image_count], attended[image_count:])
    results = []
    for stream in range(2):
        portion = portions[stream]
        branch = low_back(product(pieces[stream], weights[4 * stream + 1]))
        middle = hidden[stream] + portion[2] * branch
        entry_mlp = low(layer_norm(middle) * (1.0 + portion[4]) + portion[3])
        pre_gelu = low_back(product(entry_mlp, weights[4 * stream + 2]))
        active = low(jax.nn.gelu(pre_gelu, approximate=True))
        final_out = low_back(product(active, weights[4 * stream + 3]))
        results.append(middle + portion[5] * final_out)
    return results

def forward(params, image_tokens, text_tokens, condition):
    image_modulator, image_heads, image_merge, image_expand, image_reduce, text_modulator, text_heads, text_merge, text_expand, text_reduce = params
    condition_act = low(jax.nn.silu(condition))
    image_mods = low_back(jnp.einsum('sd,ldk->slk', condition_act, image_modulator, precision=HIGHEST))
    text_mods = low_back(jnp.einsum('sd,ldk->slk', condition_act, text_modulator, precision=HIGHEST))

    def one_sequence(items):
        image_hidden, text_hidden, image_mod, text_mod = items
        hidden = [image_hidden, text_hidden]
        for layer_index in range(LAYERS):
            weights = (image_heads[layer_index], image_merge[layer_index], image_expand[layer_index], image_reduce[layer_index], text_heads[layer_index], text_merge[layer_index], text_expand[layer_index], text_reduce[layer_index])
            hidden = joint_layer(hidden, (image_mod[layer_index], text_mod[layer_index]), weights)
        return (hidden[0], hidden[1])
    return lax.map(jax.checkpoint(one_sequence), (image_tokens, text_tokens, image_mods, text_mods))

def reference(image_tokens, text_tokens, condition, occupied, image_cotangent, text_cotangent, image_modulator, image_heads, image_merge, image_expand, image_reduce, text_modulator, text_heads, text_merge, text_expand, text_reduce):
    params = tuple((weight.astype(jnp.float32) for weight in (image_modulator, image_heads, image_merge, image_expand, image_reduce, text_modulator, text_heads, text_merge, text_expand, text_reduce)))
    occupancy = occupied.astype(jnp.float32)[:, None, None]
    outputs, pull_back = jax.vjp(forward, params, image_tokens.astype(jnp.float32), text_tokens.astype(jnp.float32), condition.astype(jnp.float32))
    param_grads, image_grad, text_grad, condition_grad = pull_back((image_cotangent.astype(jnp.float32) * occupancy, text_cotangent.astype(jnp.float32) * occupancy))
    return ((outputs[0] * occupancy).astype(jnp.bfloat16), (outputs[1] * occupancy).astype(jnp.bfloat16), image_grad.astype(jnp.bfloat16), text_grad.astype(jnp.bfloat16), condition_grad, param_grads[0], param_grads[1], param_grads[2], param_grads[3], param_grads[4], param_grads[5], param_grads[6], param_grads[7], param_grads[8], param_grads[9])
```

```python
import jax
import jax.numpy as jnp
from jax import lax
from jax.experimental import pallas as pl
from jax.experimental.pallas import tpu as pltpu
from jax.sharding import PartitionSpec as P

HEAD_DIM = 64


EPSILON = 1e-06


def layer_norm(values):
    centered = values - jnp.mean(values, axis=-1, keepdims=True)
    inverse = lax.rsqrt(jnp.mean(centered * centered, axis=-1, keepdims=True) + EPSILON)
    return (centered * inverse, inverse)


def norm_back(incoming, normed, inverse):
    mean_plain = jnp.mean(incoming, axis=-1, keepdims=True)
    mean_mixed = jnp.mean(incoming * normed, axis=-1, keepdims=True)
    return inverse * (incoming - mean_plain - normed * mean_mixed)


def low(values):
    return values.astype(jnp.bfloat16)


def wide(values):
    return values.astype(jnp.float32)


def product(former, latter):
    return jnp.dot(former, latter, preferred_element_type=jnp.float32)


def product_nt(former, latter):
    return lax.dot_general(
        former, latter, (((1,), (1,)), ((), ())), preferred_element_type=jnp.float32
    )


def product_tn(former, latter):
    return lax.dot_general(
        former, latter, (((0,), (0,)), ((), ())), preferred_element_type=jnp.float32
    )


def gelu_tanh(values):
    return jax.nn.gelu(values, approximate=True)


def ring_steps(count):
    order = list(range(0, count, 2)) + list(range(count - 1, 0, -2))
    onward = [(order[i], order[(i + 1) % count]) for i in range(count)]
    return onward, [(b, a) for a, b in onward]


def ring_place(member, count):
    half = member // 2
    return jnp.where(member % 2 == 0, half, count - 1 - half)


def ring_member(place, count):
    place = lax.rem(place + count, count)
    return jnp.where(place < count // 2, 2 * place, 2 * (count - 1 - place) + 1)


def after(value, *earlier):
    return lax.optimization_barrier((value,) + earlier)[0]


class Lanes:
    def __init__(self):
        self.onward = None
        self.back = None


def gather_ring(shard, lanes, more_onward):
    count = lax.axis_size("fsdp")
    onward, back = ring_steps(count)
    me = lax.axis_index("fsdp")
    place = ring_place(me, count)
    hops_on = (count - 1 + more_onward) // 2
    hops_back = count - 1 - hops_on
    whole = jnp.zeros((count,) + shard.shape, shard.dtype)
    arrivals = []

    def put(whole, piece, member):
        return lax.dynamic_update_slice_in_dim(whole, piece[None], member, 0)

    whole = put(whole, shard, me)
    right = shard if lanes.onward is None else after(shard, lanes.onward)
    left = shard if lanes.back is None else after(shard, lanes.back)
    for step in range(1, max(hops_on, hops_back) + 1):
        came = []
        if step <= hops_on:
            right = lax.ppermute(right, "fsdp", onward)
            whole = put(whole, right, ring_member(place - step, count))
            came.append(right)
        if step <= hops_back:
            left = lax.ppermute(left, "fsdp", back)
            whole = put(whole, left, ring_member(place + step, count))
            came.append(left)
        arrivals.append(came)
    lanes.onward, lanes.back = right, left
    return whole, arrivals


def scatter_ring(terms, lanes, more_onward):
    count = lax.axis_size("fsdp")
    onward, back = ring_steps(count)
    place = ring_place(lax.axis_index("fsdp"), count)
    hops_on = (count - 1 + more_onward) // 2
    hops_back = count - 1 - hops_on
    arrivals = []

    def block(position):
        return lax.dynamic_index_in_dim(terms, ring_member(position, count), 0, keepdims=False)

    right, left = block(place + hops_on), block(place - hops_back)
    if lanes.onward is not None:
        right = after(right, lanes.onward)
        left = after(left, lanes.back)
    for step in range(1, max(hops_on, hops_back) + 1):
        came = []
        if step <= hops_on:
            right = lax.ppermute(right, "fsdp", onward)
            came.append(right)
            if step < hops_on:
                right = low(wide(right) + wide(block(place + hops_on - step)))
        if step <= hops_back:
            left = lax.ppermute(left, "fsdp", back)
            came.append(left)
            if step < hops_back:
                left = low(wide(left) + wide(block(place - hops_back + step)))
        arrivals.append(came)
    lanes.onward, lanes.back = right, left
    return low(wide(right) + wide(left) + wide(block(place))), arrivals


PARTNER = [(0, 1), (1, 0), (2, 3), (3, 2)]
ACROSS = [(0, 2), (2, 0), (1, 3), (3, 1)]


def to_partner(value):
    return lax.ppermute(value, "seq", PARTNER)


def to_across(value):
    return lax.ppermute(value, "seq", ACROSS)


def share(value):
    across = to_across(value)
    return [value, to_partner(value), across, to_partner(across)]


def share_rows(value):
    return jnp.concatenate(share(value), 0)


def fold_rows(partial):
    rows = partial.shape[0] // 4
    blocks = [partial[i * rows : (i + 1) * rows] for i in range(4)]
    for_across = low(wide(blocks[2]) + wide(to_partner(blocks[3])))
    from_across = to_across(for_across)
    return wide(blocks[0]) + wide(to_partner(blocks[1])) + wide(from_across)


def exchange_blocks(value, axis):
    mine = lax.axis_index("seq")
    width = value.shape[axis] // 4

    def block(turn):
        return lax.dynamic_slice_in_dim(value, (mine ^ turn) * width, width, axis)

    over = to_across(jnp.stack([block(2), block(3)], 0))
    return [block(0), to_partner(block(1)), over[0], to_partner(over[1])]


def in_places(pieces, axis):
    mine = lax.axis_index("seq")
    width = pieces[0].shape[axis]
    shape = list(pieces[0].shape)
    shape[axis] *= 4
    whole = jnp.zeros(shape, pieces[0].dtype)
    for turn, piece in enumerate(pieces):
        whole = lax.dynamic_update_slice_in_dim(whole, piece, (mine ^ turn) * width, axis)
    return whole


def row_tile(rows):
    return rows // 3 if rows % 48 == 0 else rows


def pick_kernel(groups, width, mine_ref, source, result):
    for number in range(4):

        @pl.when(mine_ref[0] == number)
        def _():
            for group in range(groups):
                start = (group * 4 + number) * width
                result[:, group * width : (group + 1) * width] = source[:, start : start + width]


def pick(weight, groups):
    rows, columns = weight.shape
    width = columns // groups // 4
    tile = row_tile(rows)
    mine = jnp.reshape(lax.axis_index("seq"), (1,)).astype(jnp.int32)
    return pl.pallas_call(
        lambda *refs: pick_kernel(groups, width, *refs),
        out_shape=jax.ShapeDtypeStruct((rows, groups * width), weight.dtype),
        grid_spec=pltpu.PrefetchScalarGridSpec(
            num_scalar_prefetch=1,
            grid=(rows // tile,),
            in_specs=[pl.BlockSpec((tile, columns), lambda i, mine: (i, 0))],
            out_specs=pl.BlockSpec((tile, groups * width), lambda i, mine: (i, 0)),
        ),
        cost_estimate=pl.CostEstimate(
            flops=0, bytes_accessed=4 * rows * columns, transcendentals=0
        ),
        name="pick",
    )(mine, weight)


def spread_kernel(groups, width, mine_ref, *refs):
    pieces, result = refs[:4], refs[4]
    for number in range(4):

        @pl.when(mine_ref[0] == number)
        def _():
            for group in range(groups):
                here = slice(group * width, (group + 1) * width)
                row = jnp.concatenate([pieces[number ^ place][:, here] for place in range(4)], 1)
                result[:, group * 4 * width : (group + 1) * 4 * width] = wide(row)


def spread(piece, groups):
    pieces = share(piece)
    rows, columns = piece.shape
    width = columns // groups
    tile = row_tile(rows)
    mine = jnp.reshape(lax.axis_index("seq"), (1,)).astype(jnp.int32)
    return pl.pallas_call(
        lambda *refs: spread_kernel(groups, width, *refs),
        out_shape=jax.ShapeDtypeStruct((rows, 4 * columns), jnp.float32),
        grid_spec=pltpu.PrefetchScalarGridSpec(
            num_scalar_prefetch=1,
            grid=(rows // tile,),
            in_specs=[pl.BlockSpec((tile, columns), lambda i, mine: (i, 0))] * 4,
            out_specs=pl.BlockSpec((tile, 4 * columns), lambda i, mine: (i, 0)),
        ),
        cost_estimate=pl.CostEstimate(
            flops=0, bytes_accessed=24 * rows * columns, transcendentals=0
        ),
        name="spread",
    )(mine, *pieces)[None]


def stack_kernel(mine_ref, *refs):
    pieces, result = refs[:4], refs[4]
    for number in range(4):

        @pl.when(mine_ref[0] == number)
        def _():
            for place in range(4):
                result[place] = wide(pieces[number ^ place][...])


def spread_rows(piece):
    pieces = share(piece)
    rows, columns = piece.shape
    tile = row_tile(rows)
    mine = jnp.reshape(lax.axis_index("seq"), (1,)).astype(jnp.int32)
    return pl.pallas_call(
        stack_kernel,
        out_shape=jax.ShapeDtypeStruct((4, rows, columns), jnp.float32),
        grid_spec=pltpu.PrefetchScalarGridSpec(
            num_scalar_prefetch=1,
            grid=(rows // tile,),
            in_specs=[pl.BlockSpec((tile, columns), lambda i, mine: (i, 0))] * 4,
            out_specs=pl.BlockSpec((4, tile, columns), lambda i, mine: (0, i, 0)),
        ),
        cost_estimate=pl.CostEstimate(
            flops=0, bytes_accessed=24 * rows * columns, transcendentals=0
        ),
        name="spread_rows",
    )(mine, *pieces).reshape(1, 4 * rows, columns)


def head_forward(query_head, key_head, value_head):
    scores = product_nt(query_head, key_head) * HEAD_DIM ** (-0.5)
    highest = jnp.max(scores, axis=-1, keepdims=True)
    exponent = jnp.exp(scores - highest)
    totals = jnp.sum(exponent, axis=-1, keepdims=True)
    logsum = highest + jnp.log(totals)
    output = low(product(low(exponent / totals), value_head))
    return (output, logsum)


def head_backward(query_head, key_head, value_head, output_grad, logsum):
    score_scale = HEAD_DIM ** (-0.5)
    scores = product_nt(query_head, key_head) * score_scale
    probs = jnp.exp(scores - logsum)
    probs_grad = product_nt(output_grad, value_head)
    value_grad = product_tn(low(probs), output_grad)
    scores_grad = low(probs * (probs_grad - jnp.sum(probs * probs_grad, axis=-1, keepdims=True)))
    query_grad = product(scores_grad, key_head) * score_scale
    key_grad = product_tn(scores_grad, query_head) * score_scale
    return (low(query_grad), low(key_grad), low(value_grad))


def per_device(
    image_tokens,
    text_tokens,
    condition,
    occupied,
    image_cotangent,
    text_cotangent,
    image_modulator,
    image_heads,
    image_merge,
    image_expand,
    image_reduce,
    text_modulator,
    text_heads,
    text_merge,
    text_expand,
    text_reduce,
):
    splits = lax.axis_size("seq")
    count = lax.axis_size("fsdp")
    mine = lax.axis_index("seq")
    model_width = condition.shape[1]
    own_width = model_width // count
    slab = model_width // splits
    heads_here = slab // HEAD_DIM
    hidden_width = image_expand.shape[2]
    strip = hidden_width // count // splits
    occupancy = wide(occupied)[0]
    kinds = range(2)

    raw = (
        (image_heads[0], image_merge[0], image_expand[0], image_reduce[0]),
        (text_heads[0], text_merge[0], text_expand[0], text_reduce[0]),
    )
    lanes = [Lanes(), Lanes()]

    def gather(number, share_of, *earlier):
        wholes, arrivals = [], []
        for kind in kinds:
            weight = raw[kind][number]
            if earlier:
                weight = after(weight, *earlier)
            whole, came = gather_ring(share_of(weight), lanes[kind], kind)
            wholes.append(whole)
            arrivals.append(came)
        steps = max(len(came) for came in arrivals)
        return wholes, [
            tuple(piece for came in arrivals if step < len(came) for piece in came[step])
            for step in range(steps)
        ]

    heads, heads_came = gather(0, lambda weight: pick(weight, 3))
    heads = [whole.reshape(model_width, 3 * slab) for whole in heads]
    first = heads_came[0]
    merge, merge_came = gather(
        1, lambda weight: lax.dynamic_slice_in_dim(weight, mine * slab, slab, 1), *first
    )
    expand, expand_came = gather(2, lambda weight: pick(weight, count), *first)
    expand = [whole.reshape(model_width, count * strip) for whole in expand]
    reduce, reduce_came = gather(
        3, lambda weight: lax.dynamic_slice_in_dim(weight, mine * strip, strip, 0), *first
    )
    reduce = [whole.reshape(count * strip, model_width) for whole in reduce]

    condition_value = wide(condition)
    condition_act = low(jax.nn.silu(condition_value))
    condition_slice = lax.all_to_all(
        condition_act.reshape(count, own_width), "fsdp", split_axis=0, concat_axis=0, tiled=True
    )
    modulators = (image_modulator[0], text_modulator[0])
    mod_width = modulators[0].shape[1]
    quarter = mod_width // splits
    gated_slice = after(condition_slice, *first)
    parts = jnp.stack(
        [
            product(
                gated_slice,
                lax.dynamic_slice_in_dim(modulators[kind], mine * quarter, quarter, 1),
            )
            for kind in kinds
        ],
        1,
    )
    parts = lax.all_to_all(parts, "fsdp", split_axis=0, concat_axis=0, tiled=True)
    own_quarter = after(jnp.sum(parts, axis=0), *heads_came[1])
    modulation = lax.all_gather(own_quarter, "seq", axis=0, tiled=False)
    modulation = jnp.moveaxis(modulation, 0, 1).reshape(2, mod_width)
    portions = [jnp.split(modulation[kind], 6) for kind in kinds]

    hidden = [wide(image_tokens[0]), wide(text_tokens[0])]
    first_norm = [layer_norm(hidden[kind]) for kind in kinds]
    entries = [
        share_rows(low(first_norm[kind][0] * (1.0 + portions[kind][1]) + portions[kind][0]))
        for kind in kinds
    ]
    outer_grad = [wide(image_cotangent[0]) * occupancy, wide(text_cotangent[0]) * occupancy]
    final_grad = [
        share_rows(
            after(low(outer_grad[kind] * portions[kind][5]), *heads_came[-1], *entries)
        )
        for kind in kinds
    ]
    image_rows = entries[0].shape[0]
    joined = jnp.concatenate([low(product(entries[kind], heads[kind])) for kind in kinds], 0)

    def head_of(part, number):
        start = part * slab + number * HEAD_DIM
        return joined[:, start : start + HEAD_DIM]

    outputs = []
    for number in range(heads_here):
        query = head_of(0, number)
        step = number * len(merge_came) // heads_here
        if step > 0:
            query = after(query, *merge_came[step - 1])
        outputs.append(head_forward(query, head_of(1, number), head_of(2, number)))
    attended = jnp.concatenate([output for output, _ in outputs], 1)
    pieces = (attended[:image_rows], attended[image_rows:])
    merge = [
        in_places(exchange_blocks(whole.reshape(model_width, slab), 0), 1) for whole in merge
    ]

    terms = [[None] * 4, [None] * 4]
    branch, middle, second_norm, entries_mlp = [], [], [], []
    for kind in kinds:
        piece = after(pieces[kind], *expand_came[0])
        branch.append(fold_rows(low(product(piece, merge[kind]))))
    for kind in kinds:
        branch[kind] = after(branch[kind], *expand_came[1])
        middle.append(hidden[kind] + portions[kind][2] * branch[kind])
        second_norm.append(layer_norm(middle[kind]))
        entries_mlp.append(
            share_rows(low(second_norm[kind][0] * (1.0 + portions[kind][4]) + portions[kind][3]))
        )
    summed = [[None] * 4, [None] * 4]
    back = [Lanes(), Lanes()]

    def scatter(number):
        arrivals = []
        for kind in kinds:
            term = terms[kind][number]
            summed[kind][number], came = scatter_ring(
                term.reshape(count, term.shape[0] // count, term.shape[1]), back[kind], kind
            )
            arrivals.append(came)
        steps = max(len(came) for came in arrivals)
        return [
            tuple(piece for came in arrivals if step < len(came) for piece in came[step])
            for step in range(steps)
        ]

    results, pre_grads, actives = [], [], []
    for kind in kinds:
        pre_gelu = product(entries_mlp[kind], expand[kind])
        pre_gelu = after(pre_gelu, *reduce_came[1])
        active, pull = jax.vjp(gelu_tanh, pre_gelu)
        actives.append(low(active))
        active_grad = product_nt(final_grad[kind], reduce[kind])
        pre_grads.append(low(pull(active_grad)[0]))
        terms[kind][3] = low(product_tn(actives[kind], final_grad[kind]))
    reduce_back = scatter(3)

    middle_grad, branch_grads, mod_terms = [], [], []
    for kind in kinds:
        terms[kind][2] = low(product_tn(entries_mlp[kind], pre_grads[kind]))
        entry_grad = fold_rows(low(product_nt(pre_grads[kind], expand[kind])))
        entry_grad = after(entry_grad, *reduce_back[0])
        normed, inverse = second_norm[kind]
        middle_grad.append(
            outer_grad[kind] + norm_back(entry_grad * (1.0 + portions[kind][4]), normed, inverse)
        )
        scale_two = jnp.sum(entry_grad * normed, axis=0)
        shift_two = jnp.sum(entry_grad, axis=0)
        gate_one = jnp.sum(middle_grad[kind] * branch[kind], axis=0)
        mod_terms.append((gate_one, shift_two, scale_two))
        branch_grads.append(share_rows(low(middle_grad[kind] * portions[kind][2])))
    expand_back = scatter(2)
    attended_grads = []
    for kind in kinds:
        branch_grad = after(branch_grads[kind], *reduce_back[1])
        terms[kind][1] = in_places(
            exchange_blocks(low(product_tn(pieces[kind], branch_grad)), 1), 0
        )
        attended_grads.append(low(product_nt(branch_grad, merge[kind])))
    scatter(1)
    attended_grad = jnp.concatenate(attended_grads, 0)
    came = reduce_back[2:] + expand_back
    head_grads = []
    for number in range(heads_here):
        grad = attended_grad[:, number * HEAD_DIM : (number + 1) * HEAD_DIM]
        if number > 0:
            grad = after(grad, *came[min(number, len(came)) - 1])
        head_grads.append(
            head_backward(
                head_of(0, number), head_of(1, number), head_of(2, number), grad, outputs[number][1]
            )
        )
    joined_grad = jnp.concatenate(
        [head_grads[number][part] for part in range(3) for number in range(heads_here)], 1
    )
    row_grads = (joined_grad[:image_rows], joined_grad[image_rows:])
    flowing, mod_grads = [], []
    for kind in kinds:
        terms[kind][0] = low(product_tn(entries[kind], row_grads[kind]))
    heads_back = scatter(0)
    for kind in kinds:
        final_out = fold_rows(
            low(product(after(actives[kind], *reduce_back[0]), reduce[kind]))
        )
        results.append((middle[kind] + portions[kind][5] * final_out, final_out))
        entry_grad = fold_rows(low(product_nt(row_grads[kind], heads[kind])))
        normed, inverse = first_norm[kind]
        scale_one = jnp.sum(entry_grad * normed, axis=0)
        shift_one = jnp.sum(entry_grad, axis=0)
        flowing.append(
            middle_grad[kind] + norm_back(entry_grad * (1.0 + portions[kind][1]), normed, inverse)
        )
        gate_two = jnp.sum(outer_grad[kind] * final_out, axis=0)
        gate_one, shift_two, scale_two = mod_terms[kind]
        mod_grads.append(
            jnp.concatenate([shift_one, scale_one, gate_one, shift_two, scale_two, gate_two])
        )

    grads = []
    for kind in kinds:
        heads_sum, merge_sum, expand_sum, reduce_sum = summed[kind]
        grads.append(
            (
                spread(heads_sum, 3),
                spread(merge_sum, 1),
                spread(expand_sum, count),
                spread_rows(reduce_sum),
            )
        )

    mod_partial = lax.all_gather(jnp.stack(mod_grads, 0), "seq", axis=0, tiled=False)
    mod_total = low(jnp.sum(mod_partial, axis=0)).reshape(1, 2 * mod_width)
    every = lax.all_to_all(
        jnp.broadcast_to(mod_total, (count, 2 * mod_width)),
        "fsdp",
        split_axis=0,
        concat_axis=0,
        tiled=True,
    ).reshape(count, 2, mod_width)
    mod_weights = [product_tn(condition_slice, every[:, kind])[None] for kind in kinds]
    condition_parts = product_nt(every[:, 0], modulators[0]) + product_nt(
        every[:, 1], modulators[1]
    )
    silu_grad = lax.all_to_all(
        condition_parts, "fsdp", split_axis=0, concat_axis=0, tiled=True
    ).reshape(1, model_width)
    sigmoid_value = jax.nn.sigmoid(condition_value)
    condition_grad = silu_grad * sigmoid_value * (1.0 + condition_value * (1.0 - sigmoid_value))

    return (
        low((occupancy * results[0][0])[None]),
        low((occupancy * results[1][0])[None]),
        low(flowing[0][None]),
        low(flowing[1][None]),
        condition_grad,
        mod_weights[0],
        *grads[0],
        mod_weights[1],
        *grads[1],
    )


def solution(mesh):
    rows = P("fsdp", "seq", None)
    weight = P(None, "fsdp", None)
    placed = (rows, rows, P("fsdp", None), P("fsdp"), rows, rows) + (weight,) * 10
    return jax.shard_map(
        per_device,
        mesh=mesh,
        in_specs=placed,
        out_specs=(rows, rows, rows, rows, P("fsdp", None)) + (weight,) * 10,
        check_vma=False,
    )
```
